32 devices in a mesh: lon: 4 (over y, x), lat: 4 (over z), mem: 2 (over core).
Axes of the slice: x: 2, y: 2, z: 4, core: 2. Of those that a mesh axis runs over, the one named last changes fastest.
Arguments:
- north_vel: bfloat16 [2, 4, 75, 128, 512], P('mem', None, None, 'lat', 'lon'), may hold values from -6 to 6
- up_vel: bfloat16 [2, 4, 75, 128, 512], P('mem', None, None, 'lat', 'lon'), may hold values from -6 to 6
- dens_class: int32 [2, 4, 75, 128, 512], P('mem', None, None, 'lat', 'lon'), may hold values from 0 to 79
- thickness: int32 [75, 128, 512], P(None, 'lat', 'lon'), may hold values from 0 to 2000
- basin_id: int32 [128, 512], P('lat', 'lon'), may hold values from 0 to 3
Outputs:
- depth_mean: float32 [4, 4, 2, 75, 128], P('lon', None, None, None, 'lat')
- depth_spread: float32 [4, 4, 2, 75, 128], P('lon', None, None, None, 'lat')
- class_mean: float32 [4, 4, 2, 80, 128], P('lon', None, None, None, 'lat')
- class_spread: float32 [4, 4, 2, 80, 128], P('lon', None, None, None, 'lat')
The draws below stay inside these ranges and needn't reach their ends.
Inputs may be any that keep to these rules, and one draw needn't show every extreme that they name: `basin_id`: 0 marks land; 1 to 3 name the basins. `thickness`: thousandths of a unit layer; 0 marks a cell below the sea floor.
All inputs are finite; a program needn't handle non-finite values.
Results may differ from the reference program's by a relative error of at most 0.0029.
Values sent between devices are 32-bit elements; how exact they have to be, the bound alone decides.
A program may use at most 128 MiB of HBM per device.

```python
import math
import jax
import jax.numpy as jnp
from jax import lax

MONTHS = 4
LEVELS = 75
CLASSES = 80
BASINS = 3
NLON = 512
NLAT = 128
MEMBERS = 2


def place_ends(array, rng, least, top_value):
    extent = array.shape
    index_at = [jax.random.randint(jax.random.fold_in(rng, axis), (), 0, extent[axis]) for axis in range(len(extent))]
    array = array.at[tuple(index_at)].set(least)
    longest = extent.index(max(extent))
    index_at[longest] = (index_at[longest] + 1) % extent[longest]
    return array.at[tuple(index_at)].set(top_value)


def level_of(own_key, extent, shards, low, top_value):
    factor_of, own = 1.0, jax.random.fold_in(own_key, 6)
    for position, shards_of in shards:
        heights = jnp.exp(jax.random.uniform(jax.random.fold_in(own, position), (shards_of,), jnp.float32, low / len(shards), top_value / len(shards)))
        factor_of = factor_of * jnp.repeat(heights, extent[position] // shards_of).reshape([-1 if axis == position else 1 for axis in range(len(extent))])
    return factor_of


def scatter_about(own_key, shape, width, most, pieces=(), held_as=jnp.bfloat16):
    entries = width * jax.random.normal(own_key, shape, jnp.float32)
    if pieces:
        entries = entries * level_of(own_key, shape, pieces, -0.22, 0.18)
    return jnp.clip(entries, -most, most).astype(held_as)


def setup_inputs(seed: int = 0) -> dict:
    arg_keys = jax.random.split(jax.random.key(seed), 6)
    north_vel = scatter_about(arg_keys[0], (MEMBERS, MONTHS, LEVELS, NLAT, NLON), 1.0, 6.0, ((0, 2), (3, 4), (4, 4)))
    up_vel = scatter_about(arg_keys[1], (MEMBERS, MONTHS, LEVELS, NLAT, NLON), 1.0, 6.0, ((0, 2), (3, 4), (4, 4)))
    dens_class = place_ends(jax.random.randint(arg_keys[2], (MEMBERS, MONTHS, LEVELS, NLAT, NLON), 0, CLASSES), jax.random.fold_in(arg_keys[2], 1), 0, CLASSES - 1).astype(jnp.int32)
    thickness = place_ends(jax.random.randint(arg_keys[3], (LEVELS, NLAT, NLON), 0, 2001), jax.random.fold_in(arg_keys[3], 1), 0, 2000).astype(jnp.int32)
    basin_id = place_ends(jax.random.randint(arg_keys[4], (NLAT, NLON), 0, BASINS + 1), jax.random.fold_in(arg_keys[4], 1), 0, BASINS).astype(jnp.int32)
    return {"north_vel": north_vel, "up_vel": up_vel, "dens_class": dens_class, "thickness": thickness, "basin_id": basin_id}


north_unit = 0.02
up_unit = 0.01

def class_sums(north_flux, rise_flux, dens_class, basin_masks):
    months, levels, lat_rows, lon_cells = north_flux.shape
    weighted = jnp.stack([north_flux, rise_flux], 2).reshape(months * levels, 2, lat_rows, lon_cells)
    classes_flat = dens_class.reshape(months * levels, lat_rows, lon_cells)
    class_ids = jnp.arange(CLASSES, dtype=jnp.int32)

    def one_level(packed):
        onehot = (packed[1][..., None] == class_ids).astype(jnp.float32)
        return jnp.einsum('sji,bji,jic->bscj', packed[0], basin_masks, onehot, precision=lax.Precision.HIGHEST)
    per_level = lax.map(one_level, (weighted, classes_flat))
    return lax.optimization_barrier(jnp.sum(per_level.reshape(months, levels, BASINS, 2, CLASSES, lat_rows), axis=1))

def member_tables(north_vel, up_vel, dens_class, thickness, basin_id, first_row, lat_total):
    months, levels, lat_rows, lon_cells = north_vel.shape
    row_index = first_row + jnp.arange(lat_rows, dtype=jnp.int32)
    latitude = (-78.0 + 156.0 * (row_index.astype(jnp.float32) + 0.5) / lat_total) * (math.pi / 180.0)
    zonal_width = jnp.cos(latitude)
    layer_depth = thickness.astype(jnp.float32) * 0.001
    wet_cells = (thickness > 0).astype(jnp.float32)
    north_flux = north_vel.astype(jnp.float32) * (north_unit * zonal_width)[None, None, :, None] * layer_depth[None]
    rise_flux = up_vel.astype(jnp.float32) * (up_unit * zonal_width)[None, None, :, None] * wet_cells[None]
    north_flux = north_flux.astype(jnp.bfloat16).astype(jnp.float32)
    rise_flux = rise_flux.astype(jnp.bfloat16).astype(jnp.float32)
    basin_masks = (basin_id[None] == jnp.arange(1, BASINS + 1, dtype=jnp.int32)[:, None, None]).astype(jnp.float32)
    north_depth = jnp.einsum('mkji,bji->mbkj', north_flux, basin_masks, precision=lax.Precision.HIGHEST)
    rise_depth = jnp.einsum('mkji,bji->mbkj', rise_flux, basin_masks, precision=lax.Precision.HIGHEST)
    depth_tab = jnp.stack([north_depth, rise_depth], 2)
    class_tab = class_sums(north_flux, rise_flux, dens_class, basin_masks)
    return (class_tab, depth_tab)

def with_global(tables):
    return jnp.concatenate([lax.optimization_barrier(jnp.sum(tables, axis=2, keepdims=True)), tables], 2)

def moments(stack_moc):
    members = stack_moc.shape[0]
    mean_val = lax.optimization_barrier(jnp.sum(stack_moc, 0)) / members
    spread_val = jnp.sqrt(lax.optimization_barrier(jnp.sum(jnp.square(stack_moc - mean_val), 0)) / (members - 1))
    return (mean_val, spread_val)

def reference(north_vel, up_vel, dens_class, thickness, basin_id):

    def one_member(packed):
        return member_tables(packed[0], packed[1], packed[2], thickness, basin_id, 0, NLAT)
    class_tab, depth_tab = lax.map(one_member, (north_vel, up_vel, dens_class))
    class_reg = with_global(class_tab)
    depth_reg = with_global(depth_tab)
    class_moc = jnp.stack([jnp.cumsum(class_reg[:, :, :, 0], axis=3), jnp.cumsum(jnp.cumsum(class_reg[:, :, :, 1], axis=4), axis=3)], 3)
    depth_moc = jnp.stack([jnp.cumsum(depth_reg[:, :, :, 0], axis=3), jnp.cumsum(depth_reg[:, :, :, 1], axis=4)], 3)
    depth_mean, depth_spread = moments(depth_moc)
    class_mean, class_spread = moments(class_moc)
    return (depth_mean, depth_spread, class_mean, class_spread)
```

```python
import math

import jax
import jax.numpy as jnp
from jax import lax
from jax.experimental import pallas as pl
from jax.experimental.pallas import tpu as pltpu
from jax.sharding import PartitionSpec as P

CLASSES = 80
BASINS = 3
REGIONS = BASINS + 1
LOW = 32
SUB = 8


north_unit = 0.02
up_unit = 0.01

F32, BF16 = jnp.float32, jnp.bfloat16
NT = (((1,), (1,)), ((), ()))
NN = (((1,), (0,)), ((), ()))


def round_up(n, k):
    return -(-n // k) * k


def iota(shape, axis):
    return lax.broadcasted_iota(jnp.int32, shape, axis)


def split(x):
    high = x.astype(BF16)
    return high, (x - high.astype(F32)).astype(BF16)


def exact_dot(ones, x, dims, ones_first=True):
    high, low = split(x)
    if ones_first:
        return lax.dot_general(ones, high, dims, preferred_element_type=F32) + lax.dot_general(
            ones, low, dims, preferred_element_type=F32
        )
    return lax.dot_general(high, ones, dims, preferred_element_type=F32) + lax.dot_general(
        low, ones, dims, preferred_element_type=F32
    )


def sizes_of(levels, rows):
    highs = round_up(-(-BASINS * CLASSES // LOW), 2)
    return dict(
        levels=levels,
        rows=rows,
        highs=highs,
        deep=round_up(levels, 16),
        lanes=REGIONS * rows,
        block=max(c for c in range(1, 8) if levels % c == 0),
    )


def prepare(sz, basin, consts):
    base_ref, mask_ref, upto_class, upto_level, upto_row = consts
    rows, lanes = sz["rows"], sz["lanes"]
    base_ref[...] = jnp.where(basin > 0, (basin - 1) * CLASSES, -LOW * 64)
    regions = [basin > 0] + [basin == r for r in range(1, REGIONS)]
    mask_ref[...] = jnp.concatenate(
        [jnp.where(r, 1.0, 0.0) for r in regions], axis=0
    ).astype(BF16)
    shape = upto_class.shape
    q = iota(shape, 1) // SUB
    cls = jnp.where(q < CLASSES, q, jnp.where(q < 2 * CLASSES, q - CLASSES, q - 2 * CLASSES))
    upto_class[...] = jnp.where(cls <= iota(shape, 0), 1.0, 0.0).astype(BF16)
    shape = upto_level.shape
    upto_level[...] = jnp.where(iota(shape, 1) <= iota(shape, 0), 1.0, 0.0).astype(BF16)
    shape = upto_row.shape
    a, b = iota(shape, 0), iota(shape, 1)
    upto_row[...] = jnp.where((a // rows == b // rows) & (a <= b), 1.0, 0.0).astype(BF16)


def month_tables(sz, north, up, dens, thick, coef, consts, work, put):
    base_ref, mask_ref, upto_class, upto_level, upto_row = consts
    acc, flux, depth = work
    rows, highs, levels, lanes = sz["rows"], sz["highs"], sz["levels"], sz["lanes"]
    block = sz["block"]
    acc[...] = jnp.zeros_like(acc)
    one, zero = jnp.ones((2 * SUB, 128), BF16), jnp.zeros((2 * SUB, 128), BF16)

    def step(t, carry):
        for pair in range(rows // (2 * SUB)):
            cells = slice(pair * 2 * SUB, (pair + 1) * 2 * SUB)
            lhs, rhs = ([], []), ([], [])
            for kk in range(block):
                k = t * block + kk
                depth_k = thick[k, cells, :]
                nf = north[k, cells, :].astype(F32) * coef[0, cells, :] * (
                    depth_k.astype(F32) * 0.001
                )
                rf = up[k, cells, :].astype(F32) * jnp.where(depth_k > 0, coef[1, cells, :], 0.0)
                flux[0, k, cells, :] = nf.astype(BF16)
                flux[1, k, cells, :] = rf.astype(BF16)
                q = base_ref[cells, :] + dens[k, cells, :]
                hi, lo = (q >> 5).astype(F32), (q & (LOW - 1)).astype(F32)
                for half in range(2):
                    part = slice(half * SUB, (half + 1) * SUB)
                    twin = lambda x, d: jnp.concatenate([x[part], x[part] - d], 0).astype(BF16)
                    both = lambda x: jnp.concatenate([x[part], x[part]], 0).astype(BF16)
                    hp, lp, nd, rd = twin(hi, 1.0), twin(lo, 1.0), both(nf), both(rf)
                    rhs[half].append(
                        jnp.concatenate(
                            [jnp.where(lp == BF16(2 * p), one, zero) for p in range(LOW // 2)], 0
                        )
                    )
                    hits = [hp == BF16(2 * p) for p in range(highs // 2)]
                    lhs[half].append(
                        jnp.concatenate(
                            [jnp.where(h, nd, zero) for h in hits]
                            + [jnp.where(h, rd, zero) for h in hits],
                            0,
                        )
                    )
            for half in range(2):
                acc[2 * pair + half] += lax.dot_general(
                    jnp.concatenate(lhs[half], 1),
                    jnp.concatenate(rhs[half], 1),
                    NT,
                    preferred_element_type=F32,
                )
        return carry

    lax.fori_loop(0, levels // block, step, 0)

    own = iota((SUB, LOW * SUB), 0) == iota((SUB, LOW * SUB), 1) % SUB
    q = iota((rows, highs * LOW * SUB), 1) // SUB
    row_own = iota((rows, lanes), 0) == iota((rows, lanes), 1) % rows
    for s in range(2):
        grid = jnp.concatenate(
            [
                jnp.concatenate(
                    [
                        jnp.where(own, acc[g, pl.ds((s * highs + h) * SUB, SUB), :], 0.0)
                        for h in range(highs)
                    ],
                    1,
                )
                for g in range(rows // SUB)
            ],
            0,
        )
        total = None
        for piece in split(grid):
            piece = piece.astype(F32)
            parts = [piece] + [
                jnp.where((q >= b * CLASSES) & (q < (b + 1) * CLASSES), piece, 0.0)
                for b in range(BASINS)
            ]
            term = lax.dot_general(
                upto_class[...],
                jnp.concatenate(parts, 0).astype(BF16),
                NT,
                preferred_element_type=F32,
            )
            total = term if total is None else total + term
        found = lax.dot_general(
            flux[s].reshape(levels * rows, 128), mask_ref[...], NT, preferred_element_type=F32
        )
        found = jnp.where(row_own[None], found.reshape(levels, rows, lanes), 0.0)
        depth[0:levels, :] = jnp.sum(found, axis=1)
        if s == 0:
            put(0, total)
            put(2, exact_dot(upto_level[...], depth[...], NN))
        else:
            put(1, exact_dot(upto_row[...], total, NN, False))
            put(3, exact_dot(upto_row[...], depth[...], NN, False))


def table_rows(sz):
    return [0, CLASSES, 2 * CLASSES, 2 * CLASSES + sz["deep"], 2 * (CLASSES + sz["deep"])]


def const_shapes(sz, lons):
    rows, lanes = sz["rows"], sz["lanes"]
    return [
        pltpu.VMEM((rows, lons), jnp.int32),
        pltpu.VMEM((lanes, lons), BF16),
        pltpu.VMEM((CLASSES, sz["highs"] * LOW * SUB), BF16),
        pltpu.VMEM((sz["deep"], sz["deep"]), BF16),
        pltpu.VMEM((lanes, lanes), BF16),
    ]


def work_shapes(sz, lons):
    rows = sz["rows"]
    return [
        pltpu.VMEM((rows // SUB, 2 * sz["highs"] * SUB, LOW * SUB), F32),
        pltpu.VMEM((2, sz["levels"], rows, lons), BF16),
        pltpu.VMEM((sz["deep"], sz["lanes"]), F32),
    ]


def local_tables(sz, north_vel, up_vel, dens_class, thickness, basin_id, coef):
    months, levels, rows, lons = north_vel.shape
    at = table_rows(sz)

    def kernel(north, up, dens, thick, basin, coef, out, *scratch):
        consts, work = scratch[:5], scratch[5:]

        @pl.when(pl.program_id(0) == 0)
        def _():
            prepare(sz, basin[...], consts)
            work[2][...] = jnp.zeros_like(work[2])

        def put(i, x):
            out[0, at[i] : at[i + 1], :] = x

        month_tables(
            sz, north.at[0], up.at[0], dens.at[0], thick, coef, consts, work, put
        )

    month = pl.BlockSpec((1, levels, rows, lons), lambda m: (m, 0, 0, 0))
    whole = lambda a: pl.BlockSpec(a.shape, lambda m: (0,) * a.ndim)
    return pl.pallas_call(
        kernel,
        grid=(months,),
        out_shape=jax.ShapeDtypeStruct((months, at[-1], sz["lanes"]), F32),
        in_specs=[month, month, month, whole(thickness), whole(basin_id), whole(coef)],
        out_specs=pl.BlockSpec((1, at[-1], sz["lanes"]), lambda m: (m, 0, 0)),
        scratch_shapes=const_shapes(sz, lons) + work_shapes(sz, lons),
        compiler_params=pltpu.CompilerParams(
            dimension_semantics=("arbitrary",), vmem_limit_bytes=60 * 2**20
        ),
    )(north_vel, up_vel, dens_class, thickness, basin_id, coef)


def coefficients(rows, lons):
    first = lax.axis_index("lat") * rows
    total = rows * lax.axis_size("lat")
    row_index = first + jnp.arange(rows, dtype=jnp.int32)
    latitude = (-78.0 + 156.0 * (row_index.astype(F32) + 0.5) / total) * (math.pi / 180.0)
    width = jnp.cos(latitude)
    coef = jnp.stack([north_unit * width, up_unit * width])
    return jnp.broadcast_to(coef[:, :, None], (2, rows, lons))


def body(north_vel, up_vel, dens_class, thickness, basin_id):
    _, months, levels, rows, lons = north_vel.shape
    sz = sizes_of(levels, rows)
    at = table_rows(sz)
    table = local_tables(
        sz, north_vel[0], up_vel[0], dens_class[0], thickness, basin_id, coefficients(rows, lons)
    )
    table = lax.psum_scatter(table, "lon", scatter_dimension=0, tiled=True)
    own, lanes = table.shape[0], table.shape[-1]
    split_up = lambda i, n: jnp.moveaxis(
        table[:, at[i] : at[i] + n].reshape(own, n, REGIONS, rows), 2, 1
    )
    cn, cr = split_up(0, CLASSES), split_up(1, CLASSES)
    dn, dr = split_up(2, levels), split_up(3, levels)
    ends = lax.all_gather(jnp.concatenate([cr[..., -1], dr[..., -1]], 2), "lat")
    south = jnp.arange(ends.shape[0]) < lax.axis_index("lat")
    carry = jnp.sum(jnp.where(south[:, None, None, None], ends, 0.0), 0)
    cr = cr + carry[:, :, :CLASSES, None]
    dr = dr + carry[:, :, CLASSES:, None]
    moc = jnp.concatenate([jnp.stack([cn, cr], 2), jnp.stack([dn, dr], 2)], 3)
    members = lax.axis_size("mem")
    mean = lax.psum(moc, "mem") / members
    spread = jnp.sqrt(lax.psum(jnp.square(moc - mean), "mem") / (members - 1))
    return (
        mean[..., CLASSES:, :],
        spread[..., CLASSES:, :],
        mean[..., :CLASSES, :],
        spread[..., :CLASSES, :],
    )


def solution(mesh):
    in_specs = (
        P("mem", None, None, "lat", "lon"),
        P("mem", None, None, "lat", "lon"),
        P("mem", None, None, "lat", "lon"),
        P(None, "lat", "lon"),
        P("lat", "lon"),
    )
    out_specs = (P("lon", None, None, None, "lat"),) * 4
    return jax.shard_map(body, mesh=mesh, in_specs=in_specs, out_specs=out_specs, check_vma=False)
```

```python
import math

import jax
import jax.numpy as jnp
from jax import lax
from jax.experimental import pallas as pl
from jax.experimental.pallas import tpu as pltpu
from jax.sharding import PartitionSpec as P

CLASSES = 80
BASINS = 3
REGIONS = BASINS + 1
LOW = 32
SUB = 8


north_unit = 0.02
up_unit = 0.01

F32, BF16 = jnp.float32, jnp.bfloat16
NT = (((1,), (1,)), ((), ()))
NN = (((1,), (0,)), ((), ()))


def round_up(n, k):
    return -(-n // k) * k


def iota(shape, axis):
    return lax.broadcasted_iota(jnp.int32, shape, axis)


def split(x):
    high = x.astype(BF16)
    return high, (x - high.astype(F32)).astype(BF16)


def exact_dot(ones, x, dims, ones_first=True):
    high, low = split(x)
    if ones_first:
        return lax.dot_general(ones, high, dims, preferred_element_type=F32) + lax.dot_general(
            ones, low, dims, preferred_element_type=F32
        )
    return lax.dot_general(high, ones, dims, preferred_element_type=F32) + lax.dot_general(
        low, ones, dims, preferred_element_type=F32
    )


def sizes_of(levels, rows):
    highs = round_up(-(-BASINS * CLASSES // LOW), 2)
    return dict(
        levels=levels,
        rows=rows,
        highs=highs,
        deep=round_up(levels, 16),
        lanes=REGIONS * rows,
        block=max(c for c in range(1, 8) if levels % c == 0),
    )


def prepare(sz, basin, consts):
    base_ref, mask_ref, upto_class, upto_level, upto_row = consts
    rows, lanes = sz["rows"], sz["lanes"]
    base_ref[...] = jnp.where(basin > 0, (basin - 1) * CLASSES, -LOW * 64)
    regions = [basin > 0] + [basin == r for r in range(1, REGIONS)]
    mask_ref[...] = jnp.concatenate(
        [jnp.where(r, 1.0, 0.0) for r in regions], axis=0
    ).astype(BF16)
    shape = upto_class.shape
    q = iota(shape, 1) // SUB
    cls = jnp.where(q < CLASSES, q, jnp.where(q < 2 * CLASSES, q - CLASSES, q - 2 * CLASSES))
    upto_class[...] = jnp.where(cls <= iota(shape, 0), 1.0, 0.0).astype(BF16)
    shape = upto_level.shape
    upto_level[...] = jnp.where(iota(shape, 1) <= iota(shape, 0), 1.0, 0.0).astype(BF16)
    shape = upto_row.shape
    a, b = iota(shape, 0), iota(shape, 1)
    upto_row[...] = jnp.where((a // rows == b // rows) & (a <= b), 1.0, 0.0).astype(BF16)


def month_tables(sz, north, up, dens, thick, coef, consts, work, put):
    base_ref, mask_ref, upto_class, upto_level, upto_row = consts
    acc, flux, depth = work
    rows, highs, levels, lanes = sz["rows"], sz["highs"], sz["levels"], sz["lanes"]
    block = sz["block"]
    acc[...] = jnp.zeros_like(acc)
    one, zero = jnp.ones((2 * SUB, 128), BF16), jnp.zeros((2 * SUB, 128), BF16)

    def step(t, carry):
        for pair in range(rows // (2 * SUB)):
            cells = slice(pair * 2 * SUB, (pair + 1) * 2 * SUB)
            lhs, rhs = ([], []), ([], [])
            for kk in range(block):
                k = t * block + kk
                depth_k = thick[k, cells, :]
                nf = north[k, cells, :].astype(F32) * coef[0, cells, :] * (
                    depth_k.astype(F32) * 0.001
                )
                rf = up[k, cells, :].astype(F32) * jnp.where(depth_k > 0, coef[1, cells, :], 0.0)
                flux[0, k, cells, :] = nf.astype(BF16)
                flux[1, k, cells, :] = rf.astype(BF16)
                q = base_ref[cells, :] + dens[k, cells, :]
                hi, lo = (q >> 5).astype(F32), (q & (LOW - 1)).astype(F32)
                for half in range(2):
                    part = slice(half * SUB, (half + 1) * SUB)
                    twin = lambda x, d: jnp.concatenate([x[part], x[part] - d], 0).astype(BF16)
                    both = lambda x: jnp.concatenate([x[part], x[part]], 0).astype(BF16)
                    hp, lp, nd, rd = twin(hi, 1.0), twin(lo, 1.0), both(nf), both(rf)
                    rhs[half].append(
                        jnp.concatenate(
                            [jnp.where(lp == BF16(2 * p), one, zero) for p in range(LOW // 2)], 0
                        )
                    )
                    hits = [hp == BF16(2 * p) for p in range(highs // 2)]
                    lhs[half].append(
                        jnp.concatenate(
                            [jnp.where(h, nd, zero) for h in hits]
                            + [jnp.where(h, rd, zero) for h in hits],
                            0,
                        )
                    )
            for half in range(2):
                acc[2 * pair + half] += lax.dot_general(
                    jnp.concatenate(lhs[half], 1),
                    jnp.concatenate(rhs[half], 1),
                    NT,
                    preferred_element_type=F32,
                )
        return carry

    lax.fori_loop(0, levels // block, step, 0)

    own = iota((SUB, LOW * SUB), 0) == iota((SUB, LOW * SUB), 1) % SUB
    q = iota((rows, highs * LOW * SUB), 1) // SUB
    row_own = iota((rows, lanes), 0) == iota((rows, lanes), 1) % rows
    for s in range(2):
        grid = jnp.concatenate(
            [
                jnp.concatenate(
                    [
                        jnp.where(own, acc[g, pl.ds((s * highs + h) * SUB, SUB), :], 0.0)
                        for h in range(highs)
                    ],
                    1,
                )
                for g in range(rows // SUB)
            ],
            0,
        )
        total = None
        for piece in split(grid):
            piece = piece.astype(F32)
            parts = [piece] + [
                jnp.where((q >= b * CLASSES) & (q < (b + 1) * CLASSES), piece, 0.0)
                for b in range(BASINS)
            ]
            term = lax.dot_general(
                upto_class[...],
                jnp.concatenate(parts, 0).astype(BF16),
                NT,
                preferred_element_type=F32,
            )
            total = term if total is None else total + term
        found = lax.dot_general(
            flux[s].reshape(levels * rows, 128), mask_ref[...], NT, preferred_element_type=F32
        )
        found = jnp.where(row_own[None], found.reshape(levels, rows, lanes), 0.0)
        depth[0:levels, :] = jnp.sum(found, axis=1)
        if s == 0:
            put(0, total)
            put(2, exact_dot(upto_level[...], depth[...], NN))
        else:
            put(1, exact_dot(upto_row[...], total, NN, False))
            put(3, exact_dot(upto_row[...], depth[...], NN, False))


def table_rows(sz):
    return [0, CLASSES, 2 * CLASSES, 2 * CLASSES + sz["deep"], 2 * (CLASSES + sz["deep"])]


def const_shapes(sz, lons):
    rows, lanes = sz["rows"], sz["lanes"]
    return [
        pltpu.VMEM((rows, lons), jnp.int32),
        pltpu.VMEM((lanes, lons), BF16),
        pltpu.VMEM((CLASSES, sz["highs"] * LOW * SUB), BF16),
        pltpu.VMEM((sz["deep"], sz["deep"]), BF16),
        pltpu.VMEM((lanes, lanes), BF16),
    ]


def work_shapes(sz, lons):
    rows = sz["rows"]
    return [
        pltpu.VMEM((rows // SUB, 2 * sz["highs"] * SUB, LOW * SUB), F32),
        pltpu.VMEM((2, sz["levels"], rows, lons), BF16),
        pltpu.VMEM((sz["deep"], sz["lanes"]), F32),
    ]


def fused(sz, north_vel, up_vel, dens_class, thickness, basin_id):
    _, months, levels, rows, lons = north_vel.shape
    lanes, deep = sz["lanes"], sz["deep"]
    at = table_rows(sz)
    tall = at[-1]
    ends = CLASSES + deep
    devices, lats, members = (lax.axis_size(a) for a in ("lon", "lat", "mem"))
    assert months == devices
    far = [(de, dl) for dl in range(1, lats) for de in range(members)]

    def kernel(north_h, up_h, dens_h, thick_h, basin_h, o_dm, o_ds, o_cm, o_cs, *scratch):
        consts, work, rest = scratch[:5], scratch[5:8], scratch[8:]
        (north, up, dens, thick, basin, coef, tab, inbox, mine, membox, tail, tailbox, final) = rest[:13]
        in_sem, fix_sem, send, recv, msend, mrecv, tsend, trecv = rest[13:]
        me, lat, mem = (lax.axis_index(a) for a in ("lon", "lat", "mem"))

        def inputs(t):
            month = lax.rem(me + 1 + t, devices)
            return [
                pltpu.make_async_copy(h.at[0, month], v.at[t], in_sem.at[t, i])
                for i, (h, v) in enumerate(((north_h, north), (up_h, up), (dens_h, dens)))
            ]

        fixed = [
            pltpu.make_async_copy(basin_h, basin, fix_sem.at[0]),
            pltpu.make_async_copy(thick_h, thick, fix_sem.at[1]),
        ]
        for copy in fixed + inputs(0):
            copy.start()
        for t in range(1, devices):
            for copy in inputs(t):
                copy.start()

        barrier = pltpu.get_barrier_semaphore()
        peers = [{"lon": lax.rem(me + d, devices)} for d in range(1, devices)]
        peers += [
            {"lat": lax.rem(lat + dl, lats), "mem": lax.rem(mem + de, members)}
            for dl in range(lats)
            for de in range(members)
            if dl or de
        ]
        for peer in peers:
            pl.semaphore_signal(
                barrier, inc=1, device_id=peer, device_id_type=pl.DeviceIdType.MESH
            )

        index = lat * rows + iota((rows, lons), 0)
        latitude = (-78.0 + 156.0 * (index.astype(F32) + 0.5) / (rows * lats)) * (math.pi / 180.0)
        width = jnp.cos(latitude)
        coef[0] = north_unit * width
        coef[1] = up_unit * width
        work[2][...] = jnp.zeros_like(work[2])
        fixed[0].wait()
        prepare(sz, basin[...], consts)
        fixed[1].wait()

        def table_copy(t):
            return pltpu.make_async_remote_copy(
                src_ref=tab.at[t],
                dst_ref=inbox.at[t],
                send_sem=send.at[t],
                recv_sem=recv.at[t],
                device_id={"lon": lax.rem(me + 1 + t, devices)},
                device_id_type=pl.DeviceIdType.MESH,
            )

        def one_month(t, carry):
            for copy in inputs(t):
                copy.wait()

            def put(i, x):
                tab[t, at[i] : at[i + 1], :] = x

            month_tables(
                sz, north.at[t], up.at[t], dens.at[t], thick, coef, consts, work, put
            )

            @pl.when(t == 0)
            def _():
                pl.semaphore_wait(barrier, len(peers))

            @pl.when(t < devices - 1)
            def _():
                table_copy(t).start()

            return carry

        lax.fori_loop(0, devices, one_month, 0)

        total = tab[devices - 1]
        for t in range(devices - 1):
            table_copy(t).wait_recv()
            total = total + inbox[t]
        mine[...] = total
        copies = [
            pltpu.make_async_remote_copy(
                src_ref=mine,
                dst_ref=membox.at[de - 1],
                send_sem=msend.at[de - 1],
                recv_sem=mrecv.at[de - 1],
                device_id={"mem": lax.rem(mem + de, members)},
                device_id_type=pl.DeviceIdType.MESH,
            )
            for de in range(1, members)
        ]
        for copy in copies:
            copy.start()

        pick = (iota((2 * SUB, lanes), 1) == iota((2 * SUB, lanes), 0) * rows + rows - 1)
        pick = jnp.where(pick, 1.0, 0.0).astype(BF16)
        rise = jnp.concatenate([mine[at[1] : at[2], :], mine[at[3] : at[4], :]], 0)
        high, low = split(rise)
        tail[...] = lax.dot_general(pick, high, NT, preferred_element_type=F32) + lax.dot_general(
            pick, low, NT, preferred_element_type=F32
        )
        tails = [
            pltpu.make_async_remote_copy(
                src_ref=tail,
                dst_ref=tailbox.at[i],
                send_sem=tsend.at[i],
                recv_sem=trecv.at[i],
                device_id={"lat": lax.rem(lat + dl, lats), "mem": lax.rem(mem + de, members)},
                device_id_type=pl.DeviceIdType.MESH,
            )
            for i, (de, dl) in enumerate(far)
        ]
        for copy in tails:
            copy.start()

        wide = (iota((2 * SUB, lanes), 1) // rows) == iota((2 * SUB, lanes), 0)
        wide = jnp.where(wide, 1.0, 0.0).astype(BF16)
        for copy in tails:
            copy.wait_recv()
        for copy in copies:
            copy.wait_recv()
        for de in range(members):
            whole = mine if de == 0 else membox.at[de - 1]
            south = jnp.zeros((2 * SUB, ends), F32)
            for i, (other, dl) in enumerate(far):
                if other == de:
                    south = south + jnp.where(lat >= dl, tailbox[i], 0.0)
            high, low = split(south)
            tn = (((0,), (0,)), ((), ()))
            carry = lax.dot_general(
                high, wide, tn, preferred_element_type=F32
            ) + lax.dot_general(low, wide, tn, preferred_element_type=F32)
            final[de, at[0] : at[1], :] = whole[at[0] : at[1], :]
            final[de, at[1] : at[2], :] = whole[at[1] : at[2], :] + carry[:CLASSES]
            final[de, at[2] : at[3], :] = whole[at[2] : at[3], :]
            final[de, at[3] : at[4], :] = whole[at[3] : at[4], :] + carry[CLASSES:]

        for s in range(2):
            for i, count, o_mean, o_spread in ((s, CLASSES, o_cm, o_cs), (2 + s, levels, o_dm, o_ds)):
                part = [final[de, at[i] : at[i + 1], :] for de in range(members)]
                mean = sum(part[1:], part[0]) / members
                square = [jnp.square(x - mean) for x in part]
                spread = jnp.sqrt(sum(square[1:], square[0]) / (members - 1))
                for r in range(REGIONS):
                    o_mean[0, r, s] = mean[:count, r * rows : (r + 1) * rows]
                    o_spread[0, r, s] = spread[:count, r * rows : (r + 1) * rows]

        for t in range(devices - 1):
            table_copy(t).wait_send()
        for copy in copies + tails:
            copy.wait_send()

    out = lambda n: jax.ShapeDtypeStruct((1, REGIONS, 2, n, rows), F32)
    slots = max(1, devices - 1)
    dma = pltpu.SemaphoreType.DMA
    return pl.pallas_call(
        kernel,
        out_shape=[out(levels), out(levels), out(CLASSES), out(CLASSES)],
        in_specs=[pl.BlockSpec(memory_space=pl.ANY)] * 5,
        out_specs=[pl.BlockSpec(memory_space=pltpu.VMEM)] * 4,
        scratch_shapes=const_shapes(sz, lons)
        + work_shapes(sz, lons)
        + [
            pltpu.VMEM((months, levels, rows, lons), north_vel.dtype),
            pltpu.VMEM((months, levels, rows, lons), up_vel.dtype),
            pltpu.VMEM((months, levels, rows, lons), dens_class.dtype),
            pltpu.VMEM((levels, rows, lons), thickness.dtype),
            pltpu.VMEM((rows, lons), basin_id.dtype),
            pltpu.VMEM((2, rows, lons), F32),
            pltpu.VMEM((devices, tall, lanes), F32),
            pltpu.VMEM((slots, tall, lanes), F32),
            pltpu.VMEM((tall, lanes), F32),
            pltpu.VMEM((members - 1, tall, lanes), F32),
            pltpu.VMEM((2 * SUB, ends), F32),
            pltpu.VMEM((len(far), 2 * SUB, ends), F32),
            pltpu.VMEM((members, tall, lanes), F32),
            dma((devices, 3)),
            dma((2,)),
            dma((slots,)),
            dma((slots,)),
            dma((members - 1,)),
            dma((members - 1,)),
            dma((len(far),)),
            dma((len(far),)),
        ],
        compiler_params=pltpu.CompilerParams(
            collective_id=0, has_side_effects=True, vmem_limit_bytes=60 * 2**20
        ),
    )(north_vel, up_vel, dens_class, thickness, basin_id)


def body(north_vel, up_vel, dens_class, thickness, basin_id):
    levels, rows = north_vel.shape[2:4]
    sz = sizes_of(levels, rows)
    return tuple(fused(sz, north_vel, up_vel, dens_class, thickness, basin_id))


def solution(mesh):
    in_specs = (
        P("mem", None, None, "lat", "lon"),
        P("mem", None, None, "lat", "lon"),
        P("mem", None, None, "lat", "lon"),
        P(None, "lat", "lon"),
        P("lat", "lon"),
    )
    out_specs = (P("lon", None, None, None, "lat"),) * 4
    return jax.shard_map(body, mesh=mesh, in_specs=in_specs, out_specs=out_specs, check_vma=False)
```

```python
import math

import jax
import jax.numpy as jnp
from jax import lax
from jax.experimental import pallas as pl
from jax.experimental.pallas import tpu as pltpu
from jax.sharding import PartitionSpec as P

CLASSES = 80
BASINS = 3
REGIONS = BASINS + 1
LOW = 16
SUB = 8


north_unit = 0.02
up_unit = 0.01

F32, BF16 = jnp.float32, jnp.bfloat16
NT = (((1,), (1,)), ((), ()))
NN = (((1,), (0,)), ((), ()))


def round_up(n, k):
    return -(-n // k) * k


def iota(shape, axis):
    return lax.broadcasted_iota(jnp.int32, shape, axis)


def split(x):
    high = x.astype(BF16)
    return high, (x - high.astype(F32)).astype(BF16)


def exact_dot(ones, x, dims, ones_first=True):
    high, low = split(x)
    if ones_first:
        return lax.dot_general(ones, high, dims, preferred_element_type=F32) + lax.dot_general(
            ones, low, dims, preferred_element_type=F32
        )
    return lax.dot_general(high, ones, dims, preferred_element_type=F32) + lax.dot_general(
        low, ones, dims, preferred_element_type=F32
    )


def sizes_of(levels, rows):
    highs = round_up(-(-BASINS * CLASSES // LOW), 2)
    return dict(
        levels=levels,
        rows=rows,
        highs=highs,
        deep=round_up(levels, 16),
        lanes=REGIONS * rows,
        block=max(c for c in range(1, 32) if levels % c == 0),
    )


def prepare(sz, basin, consts):
    base_ref, mask_ref, upto_class, upto_level, upto_row = consts
    rows, lanes = sz["rows"], sz["lanes"]
    base_ref[...] = jnp.where(basin > 0, (basin - 1) * CLASSES, -LOW * 64)
    regions = [basin > 0] + [basin == r for r in range(1, REGIONS)]
    mask_ref[...] = jnp.concatenate(
        [jnp.where(r, 1.0, 0.0) for r in regions], axis=0
    ).astype(BF16)
    shape = upto_class.shape
    q = iota(shape, 1) // SUB
    cls = jnp.where(q < CLASSES, q, jnp.where(q < 2 * CLASSES, q - CLASSES, q - 2 * CLASSES))
    upto_class[...] = jnp.where(cls <= iota(shape, 0), 1.0, 0.0).astype(BF16)
    shape = upto_level.shape
    upto_level[...] = jnp.where(iota(shape, 1) <= iota(shape, 0), 1.0, 0.0).astype(BF16)
    shape = upto_row.shape
    a, b = iota(shape, 0), iota(shape, 1)
    upto_row[...] = jnp.where((a // rows == b // rows) & (a <= b), 1.0, 0.0).astype(BF16)


def month_tables(sz, north, up, dens, thick, coef, consts, work, put):
    base_ref, mask_ref, upto_class, upto_level, upto_row = consts
    acc, flux, depth = work
    rows, highs, levels, lanes = sz["rows"], sz["highs"], sz["levels"], sz["lanes"]
    block = sz["block"]
    acc[...] = jnp.zeros_like(acc)
    one, zero = jnp.ones((2 * SUB, 128), BF16), jnp.zeros((2 * SUB, 128), BF16)

    def step(t, carry):
        for pair in range(rows // (2 * SUB)):
            cells = slice(pair * 2 * SUB, (pair + 1) * 2 * SUB)
            lhs, rhs = ([], []), ([], [])
            for kk in range(block):
                k = t * block + kk
                depth_k = thick[k, cells, :]
                nf = north[k, cells, :].astype(F32) * coef[0, cells, :] * (
                    depth_k.astype(F32) * 0.001
                )
                rf = up[k, cells, :].astype(F32) * jnp.where(depth_k > 0, coef[1, cells, :], 0.0)
                flux[0, k, cells, :] = nf.astype(BF16)
                flux[1, k, cells, :] = rf.astype(BF16)
                q = base_ref[cells, :] + dens[k, cells, :]
                hi, lo = (q >> (LOW.bit_length() - 1)).astype(F32), (q & (LOW - 1)).astype(F32)
                for half in range(2):
                    part = slice(half * SUB, (half + 1) * SUB)
                    twin = lambda x, d: jnp.concatenate([x[part], x[part] - d], 0).astype(BF16)
                    both = lambda x: jnp.concatenate([x[part], x[part]], 0).astype(BF16)
                    hp, lp, nd, rd = twin(hi, 1.0), twin(lo, 1.0), both(nf), both(rf)
                    rhs[half].append(
                        jnp.concatenate(
                            [jnp.where(lp == BF16(2 * p), one, zero) for p in range(LOW // 2)], 0
                        )
                    )
                    hits = [hp == BF16(2 * p) for p in range(highs // 2)]
                    lhs[half].append(
                        jnp.concatenate(
                            [jnp.where(h, nd, zero) for h in hits]
                            + [jnp.where(h, rd, zero) for h in hits],
                            0,
                        )
                    )
            for half in range(2):
                acc[2 * pair + half] += lax.dot_general(
                    jnp.concatenate(lhs[half], 1),
                    jnp.concatenate(rhs[half], 1),
                    NT,
                    preferred_element_type=F32,
                )
        return carry

    lax.fori_loop(0, levels // block, step, 0)

    own = iota((SUB, LOW * SUB), 0) == iota((SUB, LOW * SUB), 1) % SUB
    q = iota((rows, highs * LOW * SUB), 1) // SUB
    row_own = iota((rows, lanes), 0) == iota((rows, lanes), 1) % rows
    for s in range(2):
        grid = jnp.concatenate(
            [
                jnp.concatenate(
                    [
                        jnp.where(own, acc[g, pl.ds((s * highs + h) * SUB, SUB), :], 0.0)
                        for h in range(highs)
                    ],
                    1,
                )
                for g in range(rows // SUB)
            ],
            0,
        )
        total = None
        for piece in split(grid):
            piece = piece.astype(F32)
            parts = [piece] + [
                jnp.where((q >= b * CLASSES) & (q < (b + 1) * CLASSES), piece, 0.0)
                for b in range(BASINS)
            ]
            term = lax.dot_general(
                upto_class[...],
                jnp.concatenate(parts, 0).astype(BF16),
                NT,
                preferred_element_type=F32,
            )
            total = term if total is None else total + term
        found = lax.dot_general(
            flux[s].reshape(levels * rows, 128), mask_ref[...], NT, preferred_element_type=F32
        )
        found = jnp.where(row_own[None], found.reshape(levels, rows, lanes), 0.0)
        depth[0:levels, :] = jnp.sum(found, axis=1)
        if s == 0:
            put(0, total)
            put(2, exact_dot(upto_level[...], depth[...], NN))
        else:
            put(1, exact_dot(upto_row[...], total, NN, False))
            put(3, exact_dot(upto_row[...], depth[...], NN, False))


def table_rows(sz):
    return [0, CLASSES, 2 * CLASSES, 2 * CLASSES + sz["deep"], 2 * (CLASSES + sz["deep"])]


def const_shapes(sz, lons):
    rows, lanes = sz["rows"], sz["lanes"]
    return [
        pltpu.VMEM((rows, lons), jnp.int32),
        pltpu.VMEM((lanes, lons), BF16),
        pltpu.VMEM((CLASSES, sz["highs"] * LOW * SUB), BF16),
        pltpu.VMEM((sz["deep"], sz["deep"]), BF16),
        pltpu.VMEM((lanes, lanes), BF16),
    ]


def work_shapes(sz, lons):
    rows = sz["rows"]
    return [
        pltpu.VMEM((rows // SUB, 2 * sz["highs"] * SUB, LOW * SUB), F32),
        pltpu.VMEM((2, sz["levels"], rows, lons), BF16),
        pltpu.VMEM((sz["deep"], sz["lanes"]), F32),
    ]


def fused(sz, north_vel, up_vel, dens_class, thickness, basin_id):
    _, months, levels, rows, lons = north_vel.shape
    lanes, deep = sz["lanes"], sz["deep"]
    at = table_rows(sz)
    tall = at[-1]
    ends = CLASSES + deep
    devices, lats, members = (lax.axis_size(a) for a in ("lon", "lat", "mem"))
    assert months == devices
    far = [(de, dl) for dl in range(1, lats) for de in range(members)]

    def kernel(north_h, up_h, dens_h, thick_h, basin_h, final, *scratch):
        consts, work, rest = scratch[:5], scratch[5:8], scratch[8:]
        (north, up, dens, thick, basin, coef, tab, inbox, mine, membox, tail, tailbox) = rest[:12]
        in_sem, fix_sem, send, recv, msend, mrecv, tsend, trecv = rest[12:]
        me, lat, mem = (lax.axis_index(a) for a in ("lon", "lat", "mem"))

        def inputs(t):
            month = lax.rem(me + 1 + t, devices)
            return [
                pltpu.make_async_copy(h.at[0, month], v.at[t], in_sem.at[t, i])
                for i, (h, v) in enumerate(((north_h, north), (up_h, up), (dens_h, dens)))
            ]

        fixed = [
            pltpu.make_async_copy(basin_h, basin, fix_sem.at[0]),
            pltpu.make_async_copy(thick_h, thick, fix_sem.at[1]),
        ]
        for copy in fixed + inputs(0):
            copy.start()
        for t in range(1, devices):
            for copy in inputs(t):
                copy.start()

        barrier = pltpu.get_barrier_semaphore()
        peers = [{"lon": lax.rem(me + d, devices)} for d in range(1, devices)]
        peers += [
            {"lat": lax.rem(lat + dl, lats), "mem": lax.rem(mem + de, members)}
            for dl in range(lats)
            for de in range(members)
            if dl or de
        ]
        for peer in peers:
            pl.semaphore_signal(
                barrier, inc=1, device_id=peer, device_id_type=pl.DeviceIdType.MESH
            )

        index = lat * rows + iota((rows, lons), 0)
        latitude = (-78.0 + 156.0 * (index.astype(F32) + 0.5) / (rows * lats)) * (math.pi / 180.0)
        width = jnp.cos(latitude)
        coef[0] = north_unit * width
        coef[1] = up_unit * width
        work[2][...] = jnp.zeros_like(work[2])
        fixed[0].wait()
        prepare(sz, basin[...], consts)
        fixed[1].wait()

        def table_copy(t):
            return pltpu.make_async_remote_copy(
                src_ref=tab.at[t],
                dst_ref=inbox.at[t],
                send_sem=send.at[t],
                recv_sem=recv.at[t],
                device_id={"lon": lax.rem(me + 1 + t, devices)},
                device_id_type=pl.DeviceIdType.MESH,
            )

        def one_month(t, carry):
            for copy in inputs(t):
                copy.wait()

            def put(i, x):
                tab[t, at[i] : at[i + 1], :] = x

            month_tables(
                sz, north.at[t], up.at[t], dens.at[t], thick, coef, consts, work, put
            )

            @pl.when(t == 0)
            def _():
                pl.semaphore_wait(barrier, len(peers))

            @pl.when(t < devices - 1)
            def _():
                table_copy(t).start()

            return carry

        lax.fori_loop(0, devices, one_month, 0)

        total = tab[devices - 1]
        for t in range(devices - 1):
            table_copy(t).wait_recv()
            total = total + inbox[t]
        mine[...] = total
        copies = [
            pltpu.make_async_remote_copy(
                src_ref=mine,
                dst_ref=membox.at[de - 1],
                send_sem=msend.at[de - 1],
                recv_sem=mrecv.at[de - 1],
                device_id={"mem": lax.rem(mem + de, members)},
                device_id_type=pl.DeviceIdType.MESH,
            )
            for de in range(1, members)
        ]
        for copy in copies:
            copy.start()

        pick = (iota((2 * SUB, lanes), 1) == iota((2 * SUB, lanes), 0) * rows + rows - 1)
        pick = jnp.where(pick, 1.0, 0.0).astype(BF16)
        rise = jnp.concatenate([mine[at[1] : at[2], :], mine[at[3] : at[4], :]], 0)
        high, low = split(rise)
        tail[...] = lax.dot_general(pick, high, NT, preferred_element_type=F32) + lax.dot_general(
            pick, low, NT, preferred_element_type=F32
        )
        tails = [
            pltpu.make_async_remote_copy(
                src_ref=tail,
                dst_ref=tailbox.at[i],
                send_sem=tsend.at[i],
                recv_sem=trecv.at[i],
                device_id={"lat": lax.rem(lat + dl, lats), "mem": lax.rem(mem + de, members)},
                device_id_type=pl.DeviceIdType.MESH,
            )
            for i, (de, dl) in enumerate(far)
        ]
        for copy in tails:
            copy.start()

        wide = (iota((2 * SUB, lanes), 1) // rows) == iota((2 * SUB, lanes), 0)
        wide = jnp.where(wide, 1.0, 0.0).astype(BF16)
        for copy in tails:
            copy.wait_recv()
        for copy in copies:
            copy.wait_recv()
        for de in range(members):
            whole = mine if de == 0 else membox.at[de - 1]
            south = jnp.zeros((2 * SUB, ends), F32)
            for i, (other, dl) in enumerate(far):
                if other == de:
                    south = south + jnp.where(lat >= dl, tailbox[i], 0.0)
            high, low = split(south)
            tn = (((0,), (0,)), ((), ()))
            carry = lax.dot_general(
                high, wide, tn, preferred_element_type=F32
            ) + lax.dot_general(low, wide, tn, preferred_element_type=F32)
            final[de, at[0] : at[1], :] = whole[at[0] : at[1], :]
            final[de, at[1] : at[2], :] = whole[at[1] : at[2], :] + carry[:CLASSES]
            final[de, at[2] : at[3], :] = whole[at[2] : at[3], :]
            final[de, at[3] : at[4], :] = whole[at[3] : at[4], :] + carry[CLASSES:]

        for t in range(devices - 1):
            table_copy(t).wait_send()
        for copy in copies + tails:
            copy.wait_send()

    slots = max(1, devices - 1)
    dma = pltpu.SemaphoreType.DMA
    return pl.pallas_call(
        kernel,
        out_shape=jax.ShapeDtypeStruct((members, tall, lanes), F32),
        in_specs=[pl.BlockSpec(memory_space=pl.ANY)] * 5,
        out_specs=pl.BlockSpec(memory_space=pltpu.VMEM),
        scratch_shapes=const_shapes(sz, lons)
        + work_shapes(sz, lons)
        + [
            pltpu.VMEM((months, levels, rows, lons), north_vel.dtype),
            pltpu.VMEM((months, levels, rows, lons), up_vel.dtype),
            pltpu.VMEM((months, levels, rows, lons), dens_class.dtype),
            pltpu.VMEM((levels, rows, lons), thickness.dtype),
            pltpu.VMEM((rows, lons), basin_id.dtype),
            pltpu.VMEM((2, rows, lons), F32),
            pltpu.VMEM((devices, tall, lanes), F32),
            pltpu.VMEM((slots, tall, lanes), F32),
            pltpu.VMEM((tall, lanes), F32),
            pltpu.VMEM((members - 1, tall, lanes), F32),
            pltpu.VMEM((2 * SUB, ends), F32),
            pltpu.VMEM((len(far), 2 * SUB, ends), F32),
            dma((devices, 3)),
            dma((2,)),
            dma((slots,)),
            dma((slots,)),
            dma((members - 1,)),
            dma((members - 1,)),
            dma((len(far),)),
            dma((len(far),)),
        ],
        compiler_params=pltpu.CompilerParams(
            collective_id=0, has_side_effects=True, vmem_limit_bytes=60 * 2**20
        ),
    )(north_vel, up_vel, dens_class, thickness, basin_id)


def moments(sz, final):
    members = final.shape[0]
    at, rows, levels, lanes = table_rows(sz), sz["rows"], sz["levels"], sz["lanes"]

    def kernel(final, o_dm, o_ds, o_cm, o_cs):
        for s in range(2):
            for i, count, o_mean, o_spread in ((s, CLASSES, o_cm, o_cs), (2 + s, levels, o_dm, o_ds)):
                part = [final[de, at[i] : at[i + 1], :] for de in range(members)]
                mean = sum(part[1:], part[0]) / members
                square = [jnp.square(x - mean) for x in part]
                spread = jnp.sqrt(sum(square[1:], square[0]) / (members - 1))
                for o, x in ((o_mean, mean), (o_spread, spread)):
                    pad = round_up(x.shape[0], 128) - x.shape[0]
                    x = jnp.concatenate([x, jnp.zeros((pad, lanes), F32)], 0).T
                    for r in range(REGIONS):
                        o[0, r, s] = x[r * rows : (r + 1) * rows, :count]

    out = lambda n: jax.ShapeDtypeStruct((1, REGIONS, 2, rows, n), F32)
    outs = pl.pallas_call(
        kernel,
        out_shape=[out(levels), out(levels), out(CLASSES), out(CLASSES)],
        in_specs=[pl.BlockSpec(memory_space=pltpu.VMEM)],
        out_specs=[pl.BlockSpec(memory_space=pltpu.VMEM)] * 4,
    )(final)
    return tuple(jnp.swapaxes(x, 3, 4) for x in outs)


def body(north_vel, up_vel, dens_class, thickness, basin_id):
    levels, rows = north_vel.shape[2:4]
    sz = sizes_of(levels, rows)
    return moments(sz, fused(sz, north_vel, up_vel, dens_class, thickness, basin_id))


def solution(mesh):
    in_specs = (
        P("mem", None, None, "lat", "lon"),
        P("mem", None, None, "lat", "lon"),
        P("mem", None, None, "lat", "lon"),
        P(None, "lat", "lon"),
        P("lat", "lon"),
    )
    out_specs = (P("lon", None, None, None, "lat"),) * 4
    return jax.shard_map(body, mesh=mesh, in_specs=in_specs, out_specs=out_specs, check_vma=False)
```
